256 devices in a mesh: row: 32 (over y, x, z_hi), col: 8 (over z_lo, core).
Axes of the slice: x: 4, y: 4, z: 8 (z_hi: 2, z_lo: 4; z = z_hi * 4 + z_lo), core: 2. Of those that a mesh axis runs over, the one named last changes fastest.
Arguments:
- hamiltonian_blocks: bfloat16 [32, 8, 64, 128, 128], P('row', 'col'), may hold values from -0.046875 to 0.046875
- block_rows: int32 [32, 8, 64], P('row', 'col'), may hold values from 0 to 7, as said below
- block_cols: int32 [32, 8, 64], P('row', 'col'), may hold values from 0 to 31
- block_counts: int32 [32, 8], P('row', 'col'), may hold values from 16 to 64, as said below
- initial: float32 [32768, 128], P(('row', 'col')), may hold values from -6 to 6
- center: float32 [1], replicated, may hold values from -0.3 to 0.3
- halfwidth: float32 [1], replicated, may hold values from 1 to 1.5
Outputs:
- filtered: float32 [32768, 128], P(('row', 'col'))
The draws below stay inside these ranges and needn't reach their ends.
Inputs may be any that keep to these rules, and one draw needn't show every extreme that they name: `block_rows`: padded slots hold arbitrary values. `block_counts`: some tile is full in every draw.
All inputs are finite; a program needn't handle non-finite values.
Results may differ from the reference program's by a relative error of at most 0.0068.
Values may be sent and summed in bfloat16 or wider, within the bound.
A program may use at most 128 MiB of HBM per device.

```python
import jax
import jax.numpy as jnp
from jax import lax

ORB = 128
VECS = 128
SLAB = 1
STACK = 64
DEGREE = 3
ORDER = 32768
N_ROW = 32
N_COL = 8


def pattern_pair(key):
    folded = jax.random.fold_in(key, 7301)
    first_key, second_key = jax.random.split(folded, 2)
    shape = (N_ROW, N_COL, STACK)
    grid_row = jnp.broadcast_to(jnp.arange(N_ROW, dtype=jnp.int32)[:, None, None], shape)
    slot_index = jnp.broadcast_to(jnp.arange(STACK, dtype=jnp.int32)[None, None, :], shape)
    slot_cols = jax.random.randint(first_key, shape, 0, N_ROW * SLAB, dtype=jnp.int32)
    forced = (grid_row + N_ROW - 1) % N_ROW * SLAB + slot_cols % SLAB
    slot_cols = jnp.where(slot_index == 0, forced, slot_cols)
    slot_rows = jax.random.randint(second_key, shape, 0, N_COL * SLAB, dtype=jnp.int32)
    return (slot_rows, slot_cols)


def draw_block_rows(key, part):
    return pattern_pair(key)[0]


def draw_block_cols(key, part):
    return pattern_pair(key)[1]


def draw_block_counts(key, part):
    folded = jax.random.fold_in(key, 9127)
    count_key, full_key = jax.random.split(folded, 2)
    counts = jax.random.randint(count_key, (N_ROW * N_COL,), STACK // 4, STACK + 1, dtype=jnp.int32)
    chosen = jax.random.randint(full_key, (), 0, N_ROW * N_COL, dtype=jnp.int32)
    counts = jnp.where(jnp.arange(N_ROW * N_COL, dtype=jnp.int32) == chosen, STACK, counts)
    return counts.reshape(N_ROW, N_COL)


def block_levels(rng, shape, shards, low, largest):
    level = 1.0
    for position, blocks in shards:
        heights = jax.random.uniform(jax.random.fold_in(jax.random.fold_in(rng, 6), position), (blocks,), jnp.float32, low / len(shards), largest / len(shards))
        level = level * jnp.repeat(jnp.exp(heights), shape[position] // blocks).reshape((-1,) + (1,) * (len(shape) - 1 - position))
    return level


def gaussian(rng, shape, deviation, limit, cuts=(), held_as=jnp.bfloat16):
    drawn = jax.random.normal(rng, shape, jnp.float32) * deviation
    if len(cuts) > 0:
        drawn = block_levels(rng, shape, cuts, -0.22, 0.18) * drawn
    return jnp.clip(drawn, min=-limit, max=limit).astype(held_as)


def setup_inputs(seed: int = 0) -> dict:
    key_of = jax.random.split(jax.random.key(seed), 8)
    return {
        "hamiltonian_blocks": gaussian(key_of[0], (N_ROW, N_COL, STACK, ORB, ORB), (2 * STACK * ORB) ** -0.5, 0.046875, ((0, 32), (1, 8))),
        "block_rows": draw_block_rows(jax.random.fold_in(key_of[7], 71), 0),
        "block_cols": draw_block_cols(jax.random.fold_in(key_of[7], 71), 0),
        "block_counts": draw_block_counts(jax.random.fold_in(key_of[7], 71), 0),
        "initial": gaussian(key_of[4], (ORDER, VECS), 1.0, 6.0, ((0, 256),), jnp.float32),
        "center": jnp.clip(jax.random.uniform(key_of[5], (1,), jnp.float32, -0.3, 0.3), -0.3, 0.3),
        "halfwidth": jnp.clip(jax.random.uniform(key_of[6], (1,), jnp.float32, 1.0, 1.5), 1.0, 1.5),
    }


def reference(hamiltonian_blocks, block_rows, block_cols, block_counts, initial, center, halfwidth):
    total_blocks = SLAB * N_ROW * N_COL

    def apply_operator(panel):
        source = panel.reshape(total_blocks, ORB, VECS).astype(jnp.float32)

        def visit(carried, tile_index):
            grid_row = tile_index // N_COL
            grid_col = tile_index % N_COL
            stacked = hamiltonian_blocks[grid_row, grid_col].astype(jnp.float32)
            slot_rows = block_rows[grid_row, grid_col].astype(jnp.int32)
            slot_cols = block_cols[grid_row, grid_col].astype(jnp.int32)
            live_count = block_counts[grid_row, grid_col]
            global_rows = (grid_row * (N_COL * SLAB) + slot_rows).astype(jnp.int32)
            global_cols = (((slot_cols // SLAB) * N_COL + grid_col) * SLAB + slot_cols % SLAB).astype(jnp.int32)
            is_live = (jnp.arange(STACK, dtype=jnp.int32) < live_count).astype(jnp.float32)[:, None, None]
            forward = jnp.einsum("sab,sbv->sav", stacked, source[global_cols], precision=lax.Precision.HIGHEST) * is_live
            backward = jnp.einsum("sba,sbv->sav", stacked, source[global_rows], precision=lax.Precision.HIGHEST) * is_live
            carried = carried.at[global_rows].add(forward).at[global_cols].add(backward)
            return carried, None

        zeros = jnp.zeros((total_blocks, ORB, VECS), jnp.float32)
        result, unused = lax.scan(visit, zeros, jnp.arange(N_ROW * N_COL, dtype=jnp.int32))
        return result.reshape(total_blocks * ORB, VECS)

    previous = initial
    current = initial
    for degree_step in range(DEGREE):
        applied = apply_operator(current.astype(jnp.bfloat16))
        shifted = (applied - center[0] * current) / halfwidth[0]
        if degree_step == 0:
            following = shifted
        else:
            following = 2.0 * shifted - previous
        previous = current
        current = following
    return current
```

```python
import jax
import jax.numpy as jnp
from jax import lax
from jax.experimental import pallas as pl
from jax.experimental.pallas import tpu as pltpu
from jax.sharding import PartitionSpec as P

DEGREE = 3
RING = 4
HALVES = 2
F32 = jnp.float32
BF16 = jnp.bfloat16
MESH = pl.DeviceIdType.MESH
GROUP = 8

P2T = BF16
ZT = BF16
U1T = F32
U2T = BF16


def plan(slots, row_count, col_count):
    names = {}
    at = 0
    for name, size in (
        ("u_block", slots),
        ("u_panel", slots),
        ("u_keep", slots),
        ("u_end", row_count),
        ("l_block", slots),
        ("l_panel", slots),
        ("l_keep", slots),
        ("l_end", col_count),
    ):
        names[name] = at
        at += size
    return names


def order(key, payload, live, segments):
    slots = key.shape[0]
    slot = jnp.arange(slots, dtype=jnp.int32)
    key = jnp.where(live, key, segments)
    payload = jnp.where(live, payload, 0)
    before = (key[None, :] < key[:, None]) | (
        (key[None, :] == key[:, None]) & (slot[None, :] < slot[:, None])
    )
    rank = jnp.sum(before.astype(jnp.int32), axis=1)
    hit = (rank[None, :] == slot[:, None]).astype(jnp.int32)
    block = jnp.sum(hit * slot[None, :], axis=1)
    panel = jnp.sum(hit * payload[None, :], axis=1)
    sorted_key = jnp.sum(hit * key[None, :], axis=1)
    keep = (sorted_key == jnp.roll(sorted_key, 1)) & (slot > 0)
    segment = jnp.arange(segments, dtype=jnp.int32)
    upto = jnp.sum((key[None, :] <= segment[:, None]).astype(jnp.int32), axis=1)
    have = jnp.sum((key[None, :] == segment[:, None]).astype(jnp.int32), axis=1)
    end = jnp.where(have > 0, upto, 0)
    return [block, panel, keep.astype(jnp.int32), end]


def kernel(
    at,
    meta,
    center,
    halfwidth,
    blocks_hbm,
    initial,
    out,
    blocks,
    current,
    previous,
    col0,
    col1,
    col2,
    row0,
    row1,
    row2,
    ups,
    lows,
    lsend,
    comb,
    r1opp,
    r1,
    msum,
    msend,
    r2,
    zsend,
    rz,
    usend1,
    ru1,
    usend2,
    ru2,
    load_sem,
    ssem,
    rsem,
):
    slots = blocks.shape[0]
    half = current.shape[0] // 2
    grid_row = lax.axis_index("row")
    grid_col = lax.axis_index("col")
    core = grid_col % 2
    zl = grid_col // 2
    zh = grid_row % HALVES
    x = grid_row // HALVES % RING
    y = grid_row // (HALVES * RING)
    a = x * (1 - core) + y * core
    b = y * (1 - core) + x * core

    def place(da=0, db=0, dh=0, dz=0):
        pa, pb = (a + da) % RING, (b + db) % RING
        px = pa * (1 - core) + pb * core
        py = pb * (1 - core) + pa * core
        return (
            (py * RING + px) * HALVES + (zh + dh) % HALVES,
            (zl + dz) % RING * 2 + core,
        )

    other_core = (grid_row, zl * 2 + 1 - core)

    load = pltpu.make_async_copy(blocks_hbm, blocks, load_sem)
    load.start()

    barrier = pltpu.get_barrier_semaphore()
    peers = [other_core, place(dh=1)]
    peers += [place(da=d) for d in (1, 2, 3)]
    peers += [place(db=d) for d in (1, 2, 3)]
    peers += [place(dz=d) for d in (1, 2, 3)]
    for peer in peers:
        pl.semaphore_signal(barrier, inc=1, device_id=peer, device_id_type=MESH)
    current[...] = initial[...]
    ups[0] = jnp.zeros_like(initial)
    lows[0] = jnp.zeros_like(initial)
    pl.semaphore_wait(barrier, len(peers))

    ids = {}
    sent = []

    def copy(s, name, src, dst, device):
        index = ids.setdefault(name, len(ids))
        return pltpu.make_async_remote_copy(
            src_ref=src,
            dst_ref=dst,
            send_sem=ssem.at[s, index],
            recv_sem=rsem.at[s, index],
            device_id=device,
            device_id_type=MESH,
        )

    def slot_of(da=0, db=0, dh=0):
        return ((b + db) % RING * RING + (a + da) % RING) * HALVES + (zh + dh) % HALVES

    top, bottom = pl.ds(0, half), pl.ds(half, half)

    def step(s):
        col, row = (col0, col1, col2)[s], (row0, row1, row2)[s]

        def send(name, src, dst, device):
            sent.append((s, name, src))
            copy(s, name, src, dst, device).start()

        def wait(name, dst):
            copy(s, name, dst, dst, other_core).wait_recv()

        def panel(da=0, db=0, dh=0):
            return col.at[slot_of(da, db, dh)]

        def spread1(dh):
            for d in (2, 1, 3):
                send(f"d1.{dh}.{d}", panel(dh=dh), panel(dh=dh), place(da=d))

        def got1(dh, d):
            wait(f"d1.{dh}.{d}", panel(da=-d, dh=dh))

        def spread2(dh, d):
            for side, go in ((0, 1), (1, 3)):
                send(
                    f"d2.{dh}.{d}.{side}",
                    panel(da=-d, dh=dh),
                    panel(da=-d, dh=dh),
                    place(db=go),
                )

        def relay2(dh, d):
            for side, go, part in ((0, 1, top), (1, 3, bottom)):
                have = panel(da=-d, db=-go, dh=dh)
                wait(f"d2.{dh}.{d}.{side}", have)
                send(
                    f"far.{dh}.{d}.{side}",
                    panel(da=-d, db=-go, dh=dh).at[part],
                    have.at[part],
                    place(db=go),
                )

        def far2(dh, d):
            for side, part in ((0, top), (1, bottom)):
                wait(f"far.{dh}.{d}.{side}", panel(da=-d, db=2, dh=dh).at[part])

        def row_at(dz, which):
            return row.at[(zl + dz) % RING * 2 + which]

        def row_pass(d):
            wait(f"row.{d}", row_at(-d, core))
            send(f"pass.{d}", row_at(-d, core), row_at(-d, core), other_core)

        def low_end(ra, rb, dh):
            return meta[at["l_end"] + slot_of(ra, rb, dh)]

        def reduce1_start(dh):
            for rb in range(RING):
                far = low_end(2, rb, dh)
                lsend[s, dh, 0, rb] = lows[far, top, :].astype(BF16)
                lsend[s, dh, 1, rb] = lows[far, bottom, :].astype(BF16)
            send(f"opp.{dh}.0", lsend.at[s, dh, 0], r1opp.at[s, dh, 0], place(da=1))
            send(f"opp.{dh}.1", lsend.at[s, dh, 1], r1opp.at[s, dh, 1], place(da=3))
            for rb in range(RING):
                lsend[s, dh, 2, rb] = lows[low_end(1, rb, dh), bottom, :].astype(BF16)
                lsend[s, dh, 3, rb] = lows[low_end(3, rb, dh), top, :].astype(BF16)
            send(f"near.{dh}.0", lsend.at[s, dh, 2], r1.at[s, dh, 0, 1], place(da=1))
            send(f"near.{dh}.1", lsend.at[s, dh, 3], r1.at[s, dh, 1, 0], place(da=3))

        def reduce1_join(dh):
            for side, go, part in ((0, 1, top), (1, 3, bottom)):
                wait(f"opp.{dh}.{side}", r1opp.at[s, dh, side])
                for rb in range(RING):
                    mine = lows[low_end(go, rb, dh), part, :]
                    comb[s, dh, side, rb] = (mine + r1opp[s, dh, side, rb].astype(F32)).astype(BF16)
                send(
                    f"join.{dh}.{side}",
                    comb.at[s, dh, side],
                    r1.at[s, dh, side, side],
                    place(da=go),
                )

        def reduce1_end(dh):
            wait(f"near.{dh}.0", r1.at[s, dh, 0, 1])
            wait(f"near.{dh}.1", r1.at[s, dh, 1, 0])
            wait(f"join.{dh}.0", r1.at[s, dh, 0, 0])
            wait(f"join.{dh}.1", r1.at[s, dh, 1, 1])
            for rb in (2, 1, 3, 0):
                mine = low_end(0, rb, dh)
                for which, part in ((0, top), (1, bottom)):
                    total = (
                        lows[mine, part, :]
                        + r1[s, dh, 0, which, rb].astype(F32)
                        + r1[s, dh, 1, which, rb].astype(F32)
                    )
                    if rb == 0:
                        msum[dh, part, :] = total
                    else:
                        msend[s, dh, rb - 1, part, :] = total.astype(P2T)
                if rb:
                    send(
                        f"mid.{dh}.{rb}",
                        msend.at[s, dh, rb - 1],
                        r2.at[s, dh, rb - 1],
                        place(db=rb),
                    )

        def reduce2_end(dh):
            total = msum[dh]
            for rb in (1, 3, 2):
                wait(f"mid.{dh}.{rb}", r2.at[s, dh, rb - 1])
                total = total + r2[s, dh, rb - 1].astype(F32)
            return total

        now = current[...]
        col[slot_of()] = now.astype(BF16)
        send("z", panel(), panel(), place(dh=1))
        spread1(0)
        spread2(0, 0)
        row[grid_col] = now.T.astype(BF16)
        for d in (2, 1, 3):
            send(f"row.{d}", row_at(0, core), row_at(0, core), place(dz=d))
        send("swap", row_at(0, core), row_at(0, core), other_core)

        got1(0, 1)
        spread2(0, 1)
        got1(0, 3)
        spread2(0, 3)
        relay2(0, 0)
        got1(0, 2)
        spread2(0, 2)
        row_pass(1)
        row_pass(3)
        row_pass(2)
        relay2(0, 1)
        relay2(0, 3)
        wait("z", panel(dh=1))
        spread1(1)
        spread2(1, 0)
        relay2(0, 2)
        wait("swap", row_at(0, 1 - core))
        for d in (1, 3, 2):
            wait(f"pass.{d}", row_at(-d, 1 - core))

        if s == 0:
            load.wait()

        @pl.loop(0, slots // GROUP)
        def _(g):
            total = lows[g * GROUP]
            for i in range(GROUP):
                k = g * GROUP + i
                product = jnp.dot(
                    row[meta[at["l_panel"] + k]],
                    blocks[meta[at["l_block"] + k]],
                    preferred_element_type=F32,
                )
                total = product + meta[at["l_keep"] + k].astype(F32) * total
                lows[k + 1] = total

        reduce1_start(1)
        got1(1, 1)
        spread2(1, 1)
        got1(1, 3)
        spread2(1, 3)
        relay2(1, 0)
        got1(1, 2)
        spread2(1, 2)
        reduce1_start(0)
        relay2(1, 1)
        relay2(1, 3)
        reduce1_join(1)
        relay2(1, 2)
        reduce1_join(0)
        reduce1_end(1)
        for dh in (0, 1):
            for d in (0, 1, 3, 2):
                far2(dh, d)

        @pl.loop(0, slots // GROUP)
        def _(g):
            total = ups[g * GROUP]
            for i in range(GROUP):
                k = g * GROUP + i
                product = jnp.dot(
                    blocks[meta[at["u_block"] + k]],
                    col[meta[at["u_panel"] + k]],
                    preferred_element_type=F32,
                )
                total = product + meta[at["u_keep"] + k].astype(F32) * total
                ups[k + 1] = total

        def up_end(dz, which):
            return meta[at["u_end"] + (zl + dz) % RING * 2 + which]

        for d in range(RING):
            usend1[s, d] = ups[up_end(d, 1 - core)].astype(U1T)
        send("chip", usend1.at[s], ru1.at[s], other_core)
        zsend[s] = reduce2_end(1).astype(ZT)
        send("back", zsend.at[s], rz.at[s], place(dh=1))
        reduce1_end(0)
        wait("chip", ru1.at[s])
        for d in (2, 1, 3):
            usend2[s, d - 1] = (ups[up_end(d, core)] + ru1[s, d].astype(F32)).astype(U2T)
            send(f"up.{d}", usend2.at[s, d - 1], ru2.at[s, d - 1], place(dz=d))
        upper = ups[up_end(0, core)] + ru1[s, 0].astype(F32)
        lower = reduce2_end(0)
        for d in (1, 3, 2):
            wait(f"up.{d}", ru2.at[s, d - 1])
            upper = upper + ru2[s, d - 1].astype(F32)
        wait("back", rz.at[s])
        lower = lower + rz[s].astype(F32)
        applied = upper + lower.T
        shifted = (applied - center[0] * now) / halfwidth[0]
        following = shifted if s == 0 else 2.0 * shifted - previous[...]
        previous[...] = now
        current[...] = following

    for s in range(DEGREE):
        step(s)

    for s, name, src in sent:
        copy(s, name, src, src, other_core).wait_send()

    out[...] = current[...]


def body(hamiltonian_blocks, block_rows, block_cols, block_counts, initial, center, halfwidth):
    stacked = hamiltonian_blocks[0, 0]
    slots, orbitals, _ = stacked.shape
    vectors = initial.shape[1]
    row_count = lax.axis_size("col")
    col_count = lax.axis_size("row")
    at = plan(slots, row_count, col_count)
    core = lax.axis_index("col") % 2
    rows, cols = block_rows[0, 0], block_cols[0, 0]
    live = jnp.arange(slots, dtype=jnp.int32) < block_counts[0, 0]
    chip = cols // HALVES
    turned = (chip % RING * RING + chip // RING) * HALVES + cols % HALVES
    cols = jnp.where(core == 0, cols, turned)
    meta = jnp.concatenate(
        order(rows, cols, live, row_count) + order(cols, rows, live, col_count)
    )

    steps = DEGREE
    square = (orbitals, vectors)
    part = (orbitals // 2, vectors)
    copies = 69
    vmem = pltpu.VMEM
    scratch = [
        vmem((slots, orbitals, orbitals), BF16),
        vmem(square, F32),
        vmem(square, F32),
        *[vmem((col_count,) + square, BF16)] * steps,
        *[vmem((row_count,) + square, BF16)] * steps,
        vmem((slots + 1,) + square, F32),
        vmem((slots + 1,) + square, F32),
        vmem((steps, 2, 4, RING) + part, BF16),
        vmem((steps, 2, 2, RING) + part, BF16),
        vmem((steps, 2, 2, RING) + part, BF16),
        vmem((steps, 2, 2, 2, RING) + part, BF16),
        vmem((2,) + square, F32),
        vmem((steps, 2, RING - 1) + square, P2T),
        vmem((steps, 2, RING - 1) + square, P2T),
        vmem((steps,) + square, ZT),
        vmem((steps,) + square, ZT),
        vmem((steps, RING) + square, U1T),
        vmem((steps, RING) + square, U1T),
        vmem((steps, RING - 1) + square, U2T),
        vmem((steps, RING - 1) + square, U2T),
        pltpu.SemaphoreType.DMA,
        pltpu.SemaphoreType.DMA((steps, copies)),
        pltpu.SemaphoreType.DMA((steps, copies)),
    ]
    smem = pl.BlockSpec(memory_space=pltpu.SMEM)
    whole = pl.BlockSpec(memory_space=pltpu.VMEM)

    def run(*refs):
        kernel(at, *refs)

    return pl.pallas_call(
        run,
        out_shape=jax.ShapeDtypeStruct(square, F32),
        in_specs=[smem, smem, smem, pl.BlockSpec(memory_space=pl.ANY), whole],
        out_specs=whole,
        scratch_shapes=scratch,
        compiler_params=pltpu.CompilerParams(collective_id=0, has_side_effects=True),
        name="filter",
    )(meta, center, halfwidth, stacked, initial)


def solution(mesh):
    in_specs = (
        P("row", "col", None, None, None),
        P("row", "col", None),
        P("row", "col", None),
        P("row", "col"),
        P(("row", "col"), None),
        P(),
        P(),
    )
    out_specs = P(("row", "col"), None)
    return jax.shard_map(body, mesh=mesh, in_specs=in_specs, out_specs=out_specs, check_vma=False)
```

```python
import jax
import jax.numpy as jnp
from jax import lax
from jax.experimental import pallas as pl
from jax.experimental.pallas import tpu as pltpu
from jax.sharding import PartitionSpec as P

DEGREE = 3
RING = 4
HALVES = 2
F32 = jnp.float32
BF16 = jnp.bfloat16
MESH = pl.DeviceIdType.MESH
GROUP = 32
AWAY = (2, 1, 3)

LT = BF16
MT = BF16
ZT = BF16
U1T = F32
U2T = BF16


def plan(slots, row_count, col_count):
    names = {}
    at = 0
    for name, size in (
        ("u_block", slots),
        ("u_panel", slots),
        ("u_keep", slots),
        ("u_end", row_count),
        ("l_block", slots),
        ("l_panel", slots),
        ("l_keep", slots),
        ("l_end", col_count),
    ):
        names[name] = at
        at += size
    return names


def order(key, payload, live, segments):
    slots = key.shape[0]
    slot = jnp.arange(slots, dtype=jnp.int32)
    key = jnp.where(live, key, segments)
    payload = jnp.where(live, payload, 0)
    before = (key[None, :] < key[:, None]) | (
        (key[None, :] == key[:, None]) & (slot[None, :] < slot[:, None])
    )
    rank = jnp.sum(before.astype(jnp.int32), axis=1)
    hit = (rank[None, :] == slot[:, None]).astype(jnp.int32)
    block = jnp.sum(hit * slot[None, :], axis=1)
    panel = jnp.sum(hit * payload[None, :], axis=1)
    sorted_key = jnp.sum(hit * key[None, :], axis=1)
    keep = (sorted_key == jnp.roll(sorted_key, 1)) & (slot > 0)
    segment = jnp.arange(segments, dtype=jnp.int32)
    upto = jnp.sum((key[None, :] <= segment[:, None]).astype(jnp.int32), axis=1)
    have = jnp.sum((key[None, :] == segment[:, None]).astype(jnp.int32), axis=1)
    end = jnp.where(have > 0, upto, 0)
    return [block, panel, keep.astype(jnp.int32), end]


def kernel(
    at,
    meta,
    center,
    halfwidth,
    blocks_hbm,
    initial,
    out,
    blocks,
    current,
    previous,
    col0,
    col1,
    col2,
    row0,
    row1,
    row2,
    ups,
    lows,
    lsend,
    r1,
    msum,
    msend,
    r2,
    zsend,
    rz,
    usend1,
    ru1,
    usend2,
    ru2,
    load_sem,
    ssem,
    rsem,
):
    slots = blocks.shape[0]
    grid_row = lax.axis_index("row")
    grid_col = lax.axis_index("col")
    core = grid_col % 2
    zl = grid_col // 2
    zh = grid_row % HALVES
    x = grid_row // HALVES % RING
    y = grid_row // (HALVES * RING)

    a = x * (1 - core) + y * core
    b = y * (1 - core) + x * core

    def row_of(da=0, db=0, dh=0):
        pa, pb = (a + da) % RING, (b + db) % RING
        px = pa * (1 - core) + pb * core
        py = pb * (1 - core) + pa * core
        return (py * RING + px) * HALVES + (zh + dh) % HALVES

    def place(da=0, db=0, dh=0, dz=0):
        return (row_of(da, db, dh), (zl + dz) % RING * 2 + core)

    other_core = (grid_row, zl * 2 + 1 - core)

    load = pltpu.make_async_copy(blocks_hbm, blocks, load_sem)
    load.start()

    barrier = pltpu.get_barrier_semaphore()
    peers = [other_core, place(dh=1)]
    peers += [place(da=d) for d in AWAY] + [place(db=d) for d in AWAY]
    peers += [place(dz=d) for d in AWAY]
    for peer in peers:
        pl.semaphore_signal(barrier, inc=1, device_id=peer, device_id_type=MESH)
    current[...] = initial[...]
    ups[0] = jnp.zeros_like(initial)
    lows[0] = jnp.zeros_like(initial)
    pl.semaphore_wait(barrier, len(peers))

    ids = {}
    sent = []

    def copy(s, name, src, dst, device):
        index = ids.setdefault(name, len(ids))
        return pltpu.make_async_remote_copy(
            src_ref=src,
            dst_ref=dst,
            send_sem=ssem.at[s, index],
            recv_sem=rsem.at[s, index],
            device_id=device,
            device_id_type=MESH,
        )

    def step(s):
        col, row = (col0, col1, col2)[s], (row0, row1, row2)[s]

        def send(name, src, dst, device):
            sent.append((s, name, src))
            copy(s, name, src, dst, device).start()

        def wait(name, dst):
            copy(s, name, dst, dst, other_core).wait_recv()

        def panel(da=0, db=0, dh=0):
            return col.at[row_of(da, db, dh)]

        def spread1(dh):
            for d in AWAY:
                send(f"d1.{dh}.{d}", panel(dh=dh), panel(dh=dh), place(da=d))

        def spread2(dh, da):
            for d in AWAY:
                held = panel(da=-da, dh=dh)
                send(f"d2.{dh}.{da}.{d}", held, held, place(db=d))

        def pass2(dh, da):
            wait(f"d1.{dh}.{da}", panel(da=-da, dh=dh))
            spread2(dh, da)

        def row_at(dz, which):
            return row.at[(zl + dz) % RING * 2 + which]

        def low_end(da, db, dh):
            return meta[at["l_end"] + row_of(da, db, dh)]

        def reduce1_start(dh):
            for db in AWAY + (0,):
                for d in AWAY:
                    lsend[s, dh, db, d - 1] = lows[low_end(d, db, dh)].astype(LT)
                    send(
                        f"low.{dh}.{db}.{d}",
                        lsend.at[s, dh, db, d - 1],
                        r1.at[s, dh, db, d - 1],
                        place(da=d),
                    )

        def reduce1_end(dh, db):
            total = lows[low_end(0, db, dh)]
            for d in (1, 3, 2):
                wait(f"low.{dh}.{db}.{d}", r1.at[s, dh, db, d - 1])
                total = total + r1[s, dh, db, d - 1].astype(F32)
            if db == 0:
                msum[dh] = total
            else:
                msend[s, dh, db - 1] = total.astype(MT)
                send(f"mid.{dh}.{db}", msend.at[s, dh, db - 1], r2.at[s, dh, db - 1], place(db=db))

        def reduce2_end(dh):
            total = msum[dh]
            for d in (1, 3, 2):
                wait(f"mid.{dh}.{d}", r2.at[s, dh, d - 1])
                total = total + r2[s, dh, d - 1].astype(F32)
            return total

        now = current[...]
        col[row_of()] = now.astype(BF16)
        send("z", panel(), panel(), place(dh=1))
        row[grid_col] = now.T.astype(BF16)
        for d in (2, 1, 3):
            send(f"row.{d}", row_at(0, core), row_at(0, core), place(dz=d))
        send("swap", row_at(0, core), row_at(0, core), other_core)
        spread1(0)
        spread2(0, 0)
        pass2(0, 1)
        pass2(0, 3)
        for d in (1, 3):
            wait(f"row.{d}", row_at(-d, core))
            send(f"pass.{d}", row_at(-d, core), row_at(-d, core), other_core)
        pass2(0, 2)
        for d in (2,):
            wait(f"row.{d}", row_at(-d, core))
            send(f"pass.{d}", row_at(-d, core), row_at(-d, core), other_core)
        wait("z", panel(dh=1))
        spread1(1)
        spread2(1, 0)
        wait("swap", row_at(0, 1 - core))
        for d in (1, 3, 2):
            wait(f"pass.{d}", row_at(-d, 1 - core))
        if s == 0:
            load.wait()

        @pl.loop(0, slots // GROUP)
        def _(g):
            total = lows[g * GROUP]
            for i in range(GROUP):
                k = g * GROUP + i
                product = jnp.dot(
                    row[meta[at["l_panel"] + k]],
                    blocks[meta[at["l_block"] + k]],
                    preferred_element_type=F32,
                )
                total = product + meta[at["l_keep"] + k].astype(F32) * total
                lows[k + 1] = total

        reduce1_start(1)
        pass2(1, 1)
        pass2(1, 3)
        pass2(1, 2)
        reduce1_start(0)
        for db in AWAY + (0,):
            reduce1_end(1, db)
        for dh in (0, 1):
            for da in (0, 1, 3, 2):
                for d in (1, 3, 2):
                    wait(f"d2.{dh}.{da}.{d}", panel(-da, -d, dh))

        @pl.loop(0, slots // GROUP)
        def _(g):
            total = ups[g * GROUP]
            for i in range(GROUP):
                k = g * GROUP + i
                product = jnp.dot(
                    blocks[meta[at["u_block"] + k]],
                    col[meta[at["u_panel"] + k]],
                    preferred_element_type=F32,
                )
                total = product + meta[at["u_keep"] + k].astype(F32) * total
                ups[k + 1] = total

        def up_end(dz, which):
            return meta[at["u_end"] + (zl + dz) % RING * 2 + which]

        for d in range(RING):
            usend1[s, d] = ups[up_end(d, 1 - core)].astype(U1T)
        send("chip", usend1.at[s], ru1.at[s], other_core)
        zsend[s] = reduce2_end(1).astype(ZT)
        send("back", zsend.at[s], rz.at[s], place(dh=1))
        wait("chip", ru1.at[s])
        for d in (2, 1, 3):
            usend2[s, d - 1] = (ups[up_end(d, core)] + ru1[s, d].astype(F32)).astype(U2T)
            send(f"up.{d}", usend2.at[s, d - 1], ru2.at[s, d - 1], place(dz=d))
        upper = ups[up_end(0, core)] + ru1[s, 0].astype(F32)
        for db in AWAY + (0,):
            reduce1_end(0, db)
        lower = reduce2_end(0)
        for d in (1, 3, 2):
            wait(f"up.{d}", ru2.at[s, d - 1])
            upper = upper + ru2[s, d - 1].astype(F32)
        wait("back", rz.at[s])
        lower = lower + rz[s].astype(F32)
        applied = upper + lower.T
        shifted = (applied - center[0] * now) / halfwidth[0]
        following = shifted if s == 0 else 2.0 * shifted - previous[...]
        previous[...] = now
        current[...] = following

    for s in range(DEGREE):
        step(s)

    for s, name, src in sent:
        copy(s, name, src, src, other_core).wait_send()

    out[...] = current[...]


def body(hamiltonian_blocks, block_rows, block_cols, block_counts, initial, center, halfwidth):
    stacked = hamiltonian_blocks[0, 0]
    slots, orbitals, _ = stacked.shape
    vectors = initial.shape[1]
    row_count = lax.axis_size("col")
    col_count = lax.axis_size("row")
    at = plan(slots, row_count, col_count)
    rows, cols = block_rows[0, 0], block_cols[0, 0]
    live = jnp.arange(slots, dtype=jnp.int32) < block_counts[0, 0]
    meta = jnp.concatenate(
        order(rows, cols, live, row_count) + order(cols, rows, live, col_count)
    )

    steps = DEGREE
    square = (orbitals, vectors)
    copies = 73
    vmem = pltpu.VMEM
    scratch = [
        vmem((slots, orbitals, orbitals), BF16),
        vmem(square, F32),
        vmem(square, F32),
        *[vmem((col_count,) + square, BF16)] * steps,
        *[vmem((row_count,) + square, BF16)] * steps,
        vmem((slots + 1,) + square, F32),
        vmem((slots + 1,) + square, F32),
        vmem((steps, 2, RING, RING - 1) + square, LT),
        vmem((steps, 2, RING, RING - 1) + square, LT),
        vmem((2,) + square, F32),
        vmem((steps, 2, RING - 1) + square, MT),
        vmem((steps, 2, RING - 1) + square, MT),
        vmem((steps,) + square, ZT),
        vmem((steps,) + square, ZT),
        vmem((steps, RING) + square, U1T),
        vmem((steps, RING) + square, U1T),
        vmem((steps, RING - 1) + square, U2T),
        vmem((steps, RING - 1) + square, U2T),
        pltpu.SemaphoreType.DMA,
        pltpu.SemaphoreType.DMA((steps, copies)),
        pltpu.SemaphoreType.DMA((steps, copies)),
    ]
    smem = pl.BlockSpec(memory_space=pltpu.SMEM)
    whole = pl.BlockSpec(memory_space=pltpu.VMEM)

    def run(*refs):
        kernel(at, *refs)

    return pl.pallas_call(
        run,
        out_shape=jax.ShapeDtypeStruct(square, F32),
        in_specs=[smem, smem, smem, pl.BlockSpec(memory_space=pl.ANY), whole],
        out_specs=whole,
        scratch_shapes=scratch,
        compiler_params=pltpu.CompilerParams(collective_id=0, has_side_effects=True),
        name="filter",
    )(meta, center, halfwidth, stacked, initial)


def solution(mesh):
    in_specs = (
        P("row", "col", None, None, None),
        P("row", "col", None),
        P("row", "col", None),
        P("row", "col"),
        P(("row", "col"), None),
        P(),
        P(),
    )
    out_specs = P(("row", "col"), None)
    return jax.shard_map(body, mesh=mesh, in_specs=in_specs, out_specs=out_specs, check_vma=False)
```

```python
import jax
import jax.numpy as jnp
from jax import lax
from jax.experimental import pallas as pl
from jax.experimental.pallas import tpu as pltpu
from jax.sharding import PartitionSpec as P

DEGREE = 3
RING = 4
HALVES = 2
F32 = jnp.float32
BF16 = jnp.bfloat16
MESH = pl.DeviceIdType.MESH
GROUP = 32
AWAY = (2, 1, 3)

LT = BF16
MT = BF16
ZT = BF16
U1T = F32
U2T = BF16


U_BLOCK, U_PANEL, U_KEEP, U_END, L_BLOCK, L_PANEL, L_KEEP, L_END = range(8)


def order(key, payload, live, segments):
    slots = key.shape[1]
    square = (slots, slots)
    lane = lax.broadcasted_iota(jnp.int32, square, 1)
    slot = lax.broadcasted_iota(jnp.int32, square, 0)

    def upright(v):
        return jnp.sum(jnp.where(lane == slot, v, 0), axis=1, keepdims=True)

    def flat(mask, v):
        return jnp.sum(jnp.where(mask, v, 0), axis=0, keepdims=True)

    key = jnp.where(live, key, segments)
    payload = upright(jnp.where(live, payload, 0))
    mine = upright(key)
    before = (key < mine) | ((key == mine) & (lane < slot))
    rank = jnp.sum(before.astype(jnp.int32), axis=1, keepdims=True)
    hit = rank == lane
    keep = (flat(hit, mine) == flat(rank + 1 == lane, mine)) & (lane[:1] > 0)
    upto = flat(mine <= lane, 1)
    have = flat(mine == lane, 1)
    return [flat(hit, slot), flat(hit, payload), keep.astype(jnp.int32), jnp.where(have > 0, upto, 0)]


def kernel(
    counts,
    center,
    halfwidth,
    slot_rows,
    slot_cols,
    blocks_hbm,
    initial,
    out_shifted,
    out_previous,
    meta_vector,
    meta,
    blocks,
    current,
    previous,
    col0,
    col1,
    col2,
    row0,
    row1,
    row2,
    ups,
    lows,
    lsend,
    r1,
    msum,
    msend,
    r2,
    zsend,
    rz,
    usend1,
    ru1,
    usend2,
    ru2,
    load_sem,
    meta_sem,
    initial_sem,
    ssem,
    rsem,
    line_sem,
):
    slots, row_count, col_count = blocks.shape[0], row0.shape[0], col0.shape[0]
    grid_row = lax.axis_index("row")
    grid_col = lax.axis_index("col")
    core = grid_col % 2
    zl = grid_col // 2
    zh = grid_row % HALVES
    x = grid_row // HALVES % RING
    y = grid_row // (HALVES * RING)

    a = x * (1 - core) + y * core
    b = y * (1 - core) + x * core

    def row_of(da=0, db=0, dh=0):
        pa, pb = (a + da) % RING, (b + db) % RING
        px = pa * (1 - core) + pb * core
        py = pb * (1 - core) + pa * core
        return (py * RING + px) * HALVES + (zh + dh) % HALVES

    def place(da=0, db=0, dh=0):
        return (row_of(da, db, dh), grid_col)

    far_end = 3 * (1 - zl // 2)
    near = 1 + zl % 2
    along = (far_end, 6 - zl - far_end - near, near)

    def line(n):
        return (grid_row, along[n] * 2 + core)

    other_core = (grid_row, zl * 2 + 1 - core)

    barrier = pltpu.get_barrier_semaphore()
    peers = [other_core, place(dh=1)]
    peers += [place(da=d) for d in AWAY] + [place(db=d) for d in AWAY]
    peers += [line(n) for n in range(RING - 1)]
    for peer in peers:
        pl.semaphore_signal(barrier, inc=1, device_id=peer, device_id_type=MESH)
    first = pltpu.make_async_copy(initial, current, initial_sem)
    first.start()
    load = pltpu.make_async_copy(blocks_hbm, blocks, load_sem)
    load.start()
    nothing = jnp.zeros(current.shape, F32)
    ups[0] = nothing
    lows[0] = nothing
    live = lax.broadcasted_iota(jnp.int32, (1, slots), 1) < counts[0, 0]
    rows, cols = slot_rows[...], slot_cols[...]
    table = order(rows, cols, live, row_count) + order(cols, rows, live, col_count)
    meta_vector[...] = jnp.zeros_like(meta_vector)
    for n, entry in enumerate(table):
        meta_vector[n : n + 1, 0:slots] = entry
    order_copy = pltpu.make_async_copy(meta_vector, meta, meta_sem)
    order_copy.start()
    first.wait()
    pl.semaphore_wait(barrier, len(peers))

    send_ids, receive_ids = {}, {}

    def copy(leaves, arrives, src, dst, device, by_line=False):
        return pltpu.make_async_remote_copy(
            src_ref=src,
            dst_ref=dst,
            send_sem=ssem.at[send_ids.setdefault(leaves, len(send_ids))],
            recv_sem=line_sem.at[arrives] if by_line else rsem.at[receive_ids.setdefault(arrives, len(receive_ids))],
            device_id=device,
            device_id_type=MESH,
        )

    def wait(arrives, held, by_line=False):
        copy("z", arrives, held, held, other_core, by_line).wait_recv()

    def settle(leaves, held):
        copy(leaves, "z", held, held, other_core).wait_send()

    def settle_last(s):
        settle("mid", msend.at[s])
        settle("up", usend2.at[s])
        settle("back", zsend.at[s])

    def step(s):
        col, row = (col0, col1, col2)[s], (row0, row1, row2)[s]

        def send(leaves, arrives, src, dst, device, by_line=False):
            copy(leaves, arrives, src, dst, device, by_line).start()

        def panel(da=0, db=0, dh=0):
            return col.at[row_of(da, db, dh)]

        def spread1(dh):
            for d in AWAY:
                send("d1", f"d1.{dh}.{d}", panel(dh=dh), panel(dh=dh), place(da=d))

        def spread2(dh, da):
            for d in AWAY:
                held = panel(da=-da, dh=dh)
                send("d2", "d2", held, held, place(db=d))

        def pass2(dh, da):
            wait(f"d1.{dh}.{da}", panel(da=-da, dh=dh))
            spread2(dh, da)

        def row_at(z, which):
            return row.at[z * 2 + which]

        def row_pass(d):
            held = row_at(along[d], core)
            wait(along[d], held, True)
            send("pass", "pass", held, held, other_core)

        def low_end(da, db, dh):
            return meta[L_END, row_of(da, db, dh)]

        def reduce1_start(dh):
            for db in AWAY + (0,):
                for d in AWAY:
                    lsend[s, dh, db, d - 1] = lows[low_end(d, db, dh)].astype(LT)
                    send(
                        "low",
                        f"low.{dh}.{db}",
                        lsend.at[s, dh, db, d - 1],
                        r1.at[s, dh, db, d - 1],
                        place(da=d),
                    )

        def reduce1_end(dh, db):
            total = lows[low_end(0, db, dh)]
            wait(f"low.{dh}.{db}", r1.at[s, dh, db])
            for d in AWAY:
                total = total + r1[s, dh, db, d - 1].astype(F32)
            if db == 0:
                msum[dh] = total
            else:
                msend[s, dh, db - 1] = total.astype(MT)
                send("mid", f"mid.{dh}", msend.at[s, dh, db - 1], r2.at[s, dh, db - 1], place(db=db))

        def reduce2_end(dh):
            total = msum[dh]
            wait(f"mid.{dh}", r2.at[s, dh])
            for d in AWAY:
                total = total + r2[s, dh, d - 1].astype(F32)
            return total

        now = current[...]
        col[row_of()] = now.astype(BF16)
        send("z", "z", panel(), panel(), place(dh=1))
        row[grid_col] = now.T.astype(BF16)
        for d in range(RING - 1):
            send("row", zl, row_at(zl, core), row_at(zl, core), line(d), True)
        send("pass", "pass", row_at(zl, core), row_at(zl, core), other_core)
        spread1(0)
        spread2(0, 0)
        pass2(0, 1)
        pass2(0, 3)
        row_pass(2)
        row_pass(1)
        pass2(0, 2)
        row_pass(0)
        wait("z", panel(dh=1))
        spread1(1)
        spread2(1, 0)
        wait("pass", row.at[0:RING])
        if s:
            settle_last(s - 1)
        if s == 0:
            order_copy.wait()
            load.wait()

        @pl.loop(0, slots // GROUP)
        def _(g):
            total = lows[g * GROUP]
            for i in range(GROUP):
                k = g * GROUP + i
                product = jnp.dot(
                    row[meta[L_PANEL, k]],
                    blocks[meta[L_BLOCK, k]],
                    preferred_element_type=F32,
                )
                total = product + meta[L_KEEP, k].astype(F32) * total
                lows[k + 1] = total

        reduce1_start(1)
        pass2(1, 1)
        pass2(1, 3)
        pass2(1, 2)
        reduce1_start(0)
        for db in AWAY + (0,):
            reduce1_end(1, db)
        wait("d2", col.at[0 : 2 * RING * (RING - 1)])

        @pl.loop(0, slots // GROUP)
        def _(g):
            total = ups[g * GROUP]
            for i in range(GROUP):
                k = g * GROUP + i
                product = jnp.dot(
                    blocks[meta[U_BLOCK, k]],
                    col[meta[U_PANEL, k]],
                    preferred_element_type=F32,
                )
                total = product + meta[U_KEEP, k].astype(F32) * total
                ups[k + 1] = total

        def up_end(z, which):
            return meta[U_END, z * 2 + which]

        for d in range(RING):
            usend1[s, d] = ups[up_end(d, 1 - core)].astype(U1T)
        send("chip", "chip", usend1.at[s], ru1.at[s], other_core)
        zsend[s] = reduce2_end(1).astype(ZT)
        send("back", "back", zsend.at[s], rz.at[s], place(dh=1))
        wait("chip", ru1.at[s])
        for d in range(RING - 1):
            z = along[d]
            usend2[s, d] = (ups[up_end(z, core)] + ru1[s, z].astype(F32)).astype(U2T)
            send("up", "up", usend2.at[s, d], ru2.at[s, zl], line(d))
        upper = ups[up_end(zl, core)] + ru1[s, zl].astype(F32)
        for db in AWAY + (0,):
            reduce1_end(0, db)
        settle("z", panel())
        settle("row", row.at[0 : RING - 1])
        settle("pass", row.at[0:RING])
        settle("d1", col.at[0 : 2 * (RING - 1)])
        settle("d2", col.at[0 : 2 * RING * (RING - 1)])
        settle("low", lsend.at[s])
        settle("chip", usend1.at[s])
        lower = reduce2_end(0)
        wait("up", ru2.at[s, 0 : RING - 1])
        for d in range(RING - 1):
            upper = upper + ru2[s, along[d]].astype(F32)
        wait("back", rz.at[s])
        lower = lower + rz[s].astype(F32)
        applied = upper + lower.T
        shifted = (applied - center[0] * now) / halfwidth[0]
        if s == DEGREE - 1:
            out_shifted[...] = shifted
            out_previous[...] = previous[...]
        else:
            following = shifted if s == 0 else 2.0 * shifted - previous[...]
            previous[...] = now
            current[...] = following

    for s in range(DEGREE):
        step(s)

    settle_last(DEGREE - 1)


def body(hamiltonian_blocks, block_rows, block_cols, block_counts, initial, center, halfwidth):
    stacked = hamiltonian_blocks[0, 0]
    slots, orbitals, _ = stacked.shape
    vectors = initial.shape[1]
    row_count = lax.axis_size("col")
    col_count = lax.axis_size("row")
    steps = DEGREE
    square = (orbitals, vectors)
    vmem = pltpu.VMEM
    scratch = [
        vmem((8, 128), jnp.int32),
        pltpu.SMEM((8, 128), jnp.int32),
        vmem((slots, orbitals, orbitals), BF16),
        vmem(square, F32),
        vmem(square, F32),
        *[vmem((col_count,) + square, BF16)] * steps,
        *[vmem((row_count,) + square, BF16)] * steps,
        vmem((slots + 1,) + square, F32),
        vmem((slots + 1,) + square, F32),
        vmem((steps, 2, RING, RING - 1) + square, LT),
        vmem((steps, 2, RING, RING - 1) + square, LT),
        vmem((2,) + square, F32),
        vmem((steps, 2, RING - 1) + square, MT),
        vmem((steps, 2, RING - 1) + square, MT),
        vmem((steps,) + square, ZT),
        vmem((steps,) + square, ZT),
        vmem((steps, RING) + square, U1T),
        vmem((steps, RING) + square, U1T),
        vmem((steps, RING - 1) + square, U2T),
        vmem((steps, RING) + square, U2T),
        pltpu.SemaphoreType.DMA,
        pltpu.SemaphoreType.DMA,
        pltpu.SemaphoreType.DMA,
        pltpu.SemaphoreType.DMA((10,)),
        pltpu.SemaphoreType.DMA((24,)),
        pltpu.SemaphoreType.DMA((RING,)),
    ]
    smem = pl.BlockSpec(memory_space=pltpu.SMEM)
    whole = pl.BlockSpec(memory_space=pltpu.VMEM)

    hbm = pl.BlockSpec(memory_space=pl.ANY)
    result = jax.ShapeDtypeStruct(square, F32)
    shifted, previous = pl.pallas_call(
        kernel,
        out_shape=(result, result),
        in_specs=[smem, smem, smem, whole, whole, hbm, hbm],
        out_specs=(whole, whole),
        scratch_shapes=scratch,
        compiler_params=pltpu.CompilerParams(collective_id=0, has_side_effects=True),
        name="filter",
    )(block_counts, center, halfwidth, block_rows[0], block_cols[0], stacked, initial)
    return 2.0 * shifted - previous


def solution(mesh):
    in_specs = (
        P("row", "col", None, None, None),
        P("row", "col", None),
        P("row", "col", None),
        P("row", "col"),
        P(("row", "col"), None),
        P(),
        P(),
    )
    out_specs = P(("row", "col"), None)
    return jax.shard_map(body, mesh=mesh, in_specs=in_specs, out_specs=out_specs, check_vma=False)
```

```python
import jax
import jax.numpy as jnp
from jax import lax
from jax.experimental import pallas as pl
from jax.experimental.pallas import tpu as pltpu
from jax.sharding import PartitionSpec as P

DEGREE = 3
RING = 4
HALVES = 2
F32 = jnp.float32
BF16 = jnp.bfloat16
MESH = pl.DeviceIdType.MESH
GROUP = 32
AWAY = (2, 1, 3)

LT = BF16
MT = BF16
ZT = BF16
U1T = F32
U2T = BF16


U_BLOCK, U_PANEL, U_KEEP, U_END, L_BLOCK, L_PANEL, L_KEEP, L_END = range(8)


def order(key, payload, live, segments):
    slots = key.shape[1]
    square = (slots, slots)
    lane = lax.broadcasted_iota(jnp.int32, square, 1)
    slot = lax.broadcasted_iota(jnp.int32, square, 0)

    def upright(v):
        return jnp.sum(jnp.where(lane == slot, v, 0), axis=1, keepdims=True)

    def flat(mask, v):
        return jnp.sum(jnp.where(mask, v, 0), axis=0, keepdims=True)

    key = jnp.where(live, key, segments)
    payload = upright(jnp.where(live, payload, 0))
    mine = upright(key)
    before = (key < mine) | ((key == mine) & (lane < slot))
    rank = jnp.sum(before.astype(jnp.int32), axis=1, keepdims=True)
    hit = rank == lane
    keep = (flat(hit, mine) == flat(rank + 1 == lane, mine)) & (lane[:1] > 0)
    upto = flat(mine <= lane, 1)
    have = flat(mine == lane, 1)
    return [flat(hit, slot), flat(hit, payload), keep.astype(jnp.int32), jnp.where(have > 0, upto, 0)]


def kernel(
    counts,
    center,
    halfwidth,
    slot_rows,
    slot_cols,
    blocks_hbm,
    initial,
    out_shifted,
    out_previous,
    meta_vector,
    meta,
    blocks,
    current,
    previous,
    col0,
    col1,
    col2,
    row0,
    row1,
    row2,
    ups,
    lows,
    lsend,
    r1,
    msum,
    msend,
    r2,
    zsend,
    rz,
    usend1,
    ru1,
    usend2,
    ru2,
    load_sem,
    meta_sem,
    initial_sem,
    ssem,
    rsem,
    line_sem,
):
    slots, row_count, col_count = blocks.shape[0], row0.shape[0], col0.shape[0]
    grid_row = lax.axis_index("row")
    grid_col = lax.axis_index("col")
    core = grid_col % 2
    zl = grid_col // 2
    zh = grid_row % HALVES
    x = grid_row // HALVES % RING
    y = grid_row // (HALVES * RING)

    a = x * (1 - core) + y * core
    b = y * (1 - core) + x * core

    def row_of(da=0, db=0, dh=0):
        pa, pb = (a + da) % RING, (b + db) % RING
        px = pa * (1 - core) + pb * core
        py = pb * (1 - core) + pa * core
        return (py * RING + px) * HALVES + (zh + dh) % HALVES

    def place(da=0, db=0, dh=0):
        return (row_of(da, db, dh), grid_col)

    far_end = 3 * (1 - zl // 2)
    near = 1 + zl % 2
    along = (far_end, 6 - zl - far_end - near, near)

    def line(n):
        return (grid_row, along[n] * 2 + core)

    other_core = (grid_row, zl * 2 + 1 - core)

    barrier = pltpu.get_barrier_semaphore()
    peers = [other_core, place(dh=1)]
    peers += [place(da=d) for d in AWAY] + [place(db=d) for d in AWAY]
    peers += [line(n) for n in range(RING - 1)]
    for peer in peers:
        pl.semaphore_signal(barrier, inc=1, device_id=peer, device_id_type=MESH)
    first = pltpu.make_async_copy(initial, current, initial_sem)
    first.start()
    load = pltpu.make_async_copy(blocks_hbm, blocks, load_sem)
    load.start()
    nothing = jnp.zeros(current.shape, F32)
    ups[0] = nothing
    lows[0] = nothing
    live = lax.broadcasted_iota(jnp.int32, (1, slots), 1) < counts[0, 0]
    rows, cols = slot_rows[...], slot_cols[...]
    table = order(rows, cols, live, row_count) + order(cols, rows, live, col_count)
    meta_vector[...] = jnp.zeros_like(meta_vector)
    for n, entry in enumerate(table):
        meta_vector[n : n + 1, 0:slots] = entry
    order_copy = pltpu.make_async_copy(meta_vector, meta, meta_sem)
    order_copy.start()
    first.wait()
    pl.semaphore_wait(barrier, len(peers))

    send_ids, receive_ids = {}, {}

    def copy(leaves, arrives, src, dst, device, by_line=False):
        return pltpu.make_async_remote_copy(
            src_ref=src,
            dst_ref=dst,
            send_sem=ssem.at[send_ids.setdefault(leaves, len(send_ids))],
            recv_sem=line_sem.at[arrives] if by_line else rsem.at[receive_ids.setdefault(arrives, len(receive_ids))],
            device_id=device,
            device_id_type=MESH,
        )

    def wait(arrives, held, by_line=False):
        copy("z", arrives, held, held, other_core, by_line).wait_recv()

    def settle(leaves, held):
        copy(leaves, "z", held, held, other_core).wait_send()

    def settle_last(s):
        settle("mid", msend.at[s])
        settle("up", usend2.at[s])
        settle("back", zsend.at[s])

    def step(s):
        col, row = (col0, col1, col2)[s], (row0, row1, row2)[s]

        def send(leaves, arrives, src, dst, device, by_line=False):
            copy(leaves, arrives, src, dst, device, by_line).start()

        def panel(da=0, db=0, dh=0):
            return col.at[row_of(da, db, dh)]

        def spread1(dh):
            for d in AWAY:
                send("d1", f"d1.{dh}.{d}", panel(dh=dh), panel(dh=dh), place(da=d))

        def spread2(dh, da):
            for d in AWAY:
                held = panel(da=-da, dh=dh)
                send("d2", f"d2.{s}" if da or dh else "d2own", held, held, place(db=d))

        def pass2(dh, da):
            wait(f"d1.{dh}.{da}", panel(da=-da, dh=dh))
            spread2(dh, da)

        def row_at(z, which):
            return row.at[z * 2 + which]

        def row_pass(d):
            held = row_at(along[d], core)
            wait(along[d], held, True)
            send("pass", "pass", held, held, other_core)

        def low_end(da, db, dh):
            return meta[L_END, row_of(da, db, dh)]

        def reduce1_start(dh):
            for da in AWAY + (0,):
                for d in AWAY:
                    lsend[s, dh, da, d - 1] = lows[low_end(da, d, dh)].astype(LT)
                    send(
                        "low",
                        f"low.{dh}.{da}",
                        lsend.at[s, dh, da, d - 1],
                        r1.at[s, dh, da, d - 1],
                        place(db=d),
                    )

        def reduce1_end(dh, da):
            total = lows[low_end(da, 0, dh)]
            wait(f"low.{dh}.{da}", r1.at[s, dh, da])
            for d in AWAY:
                total = total + r1[s, dh, da, d - 1].astype(F32)
            if da == 0:
                msum[dh] = total
            else:
                msend[s, dh, da - 1] = total.astype(MT)
                send("mid", f"mid.{dh}", msend.at[s, dh, da - 1], r2.at[s, dh, da - 1], place(da=da))

        def reduce2_end(dh):
            total = msum[dh]
            wait(f"mid.{dh}", r2.at[s, dh])
            for d in AWAY:
                total = total + r2[s, dh, d - 1].astype(F32)
            return total

        now = current[...]
        col[row_of()] = now.astype(BF16)
        send("z", "z", panel(), panel(), place(dh=1))
        row[grid_col] = now.T.astype(BF16)
        for d in range(RING - 1):
            send("row", zl, row_at(zl, core), row_at(zl, core), line(d), True)
        send("pass", "pass", row_at(zl, core), row_at(zl, core), other_core)
        spread1(0)
        spread2(0, 0)
        pass2(0, 1)
        pass2(0, 3)
        row_pass(2)
        row_pass(1)
        pass2(0, 2)
        row_pass(0)
        wait("z", panel(dh=1))
        spread1(1)
        spread2(1, 0)
        wait("d2own", col.at[0 : RING - 1])
        wait("pass", row.at[0:RING])
        if s:
            settle_last(s - 1)
        if s == 0:
            order_copy.wait()
            load.wait()

        @pl.loop(0, slots // GROUP)
        def _(g):
            total = lows[g * GROUP]
            for i in range(GROUP):
                k = g * GROUP + i
                product = jnp.dot(
                    row[meta[L_PANEL, k]],
                    blocks[meta[L_BLOCK, k]],
                    preferred_element_type=F32,
                )
                total = product + meta[L_KEEP, k].astype(F32) * total
                lows[k + 1] = total

        reduce1_start(1)
        pass2(1, 1)
        pass2(1, 3)
        pass2(1, 2)
        reduce1_start(0)
        for db in AWAY + (0,):
            reduce1_end(1, db)
        wait(f"d2.{s}", col.at[0 : (2 * RING - 1) * (RING - 1)])

        @pl.loop(0, slots // GROUP)
        def _(g):
            total = ups[g * GROUP]
            for i in range(GROUP):
                k = g * GROUP + i
                product = jnp.dot(
                    blocks[meta[U_BLOCK, k]],
                    col[meta[U_PANEL, k]],
                    preferred_element_type=F32,
                )
                total = product + meta[U_KEEP, k].astype(F32) * total
                ups[k + 1] = total

        def up_end(z, which):
            return meta[U_END, z * 2 + which]

        for d in range(RING):
            usend1[s, d] = ups[up_end(d, 1 - core)].astype(U1T)
        send("chip", "chip", usend1.at[s], ru1.at[s], other_core)
        zsend[s] = reduce2_end(1).astype(ZT)
        send("back", "back", zsend.at[s], rz.at[s], place(dh=1))
        wait("chip", ru1.at[s])
        for d in range(RING - 1):
            z = along[d]
            usend2[s, d] = (ups[up_end(z, core)] + ru1[s, z].astype(F32)).astype(U2T)
            send("up", "up", usend2.at[s, d], ru2.at[s, zl], line(d))
        upper = ups[up_end(zl, core)] + ru1[s, zl].astype(F32)
        for db in AWAY + (0,):
            reduce1_end(0, db)
        settle("z", panel())
        settle("row", row.at[0 : RING - 1])
        settle("pass", row.at[0:RING])
        settle("d1", col.at[0 : 2 * (RING - 1)])
        settle("d2", col.at[0 : 2 * RING * (RING - 1)])
        settle("low", lsend.at[s])
        settle("chip", usend1.at[s])
        lower = reduce2_end(0)
        wait("up", ru2.at[s, 0 : RING - 1])
        for d in range(RING - 1):
            upper = upper + ru2[s, along[d]].astype(F32)
        wait("back", rz.at[s])
        lower = lower + rz[s].astype(F32)
        applied = upper + lower.T
        shifted = (applied - center[0] * now) / halfwidth[0]
        if s == DEGREE - 1:
            out_shifted[...] = shifted
            out_previous[...] = previous[...]
        else:
            following = shifted if s == 0 else 2.0 * shifted - previous[...]
            previous[...] = now
            current[...] = following

    for s in range(DEGREE):
        step(s)

    settle_last(DEGREE - 1)


def body(hamiltonian_blocks, block_rows, block_cols, block_counts, initial, center, halfwidth):
    stacked = hamiltonian_blocks[0, 0]
    slots, orbitals, _ = stacked.shape
    vectors = initial.shape[1]
    row_count = lax.axis_size("col")
    col_count = lax.axis_size("row")
    steps = DEGREE
    square = (orbitals, vectors)
    vmem = pltpu.VMEM
    scratch = [
        vmem((8, 128), jnp.int32),
        pltpu.SMEM((8, 128), jnp.int32),
        vmem((slots, orbitals, orbitals), BF16),
        vmem(square, F32),
        vmem(square, F32),
        *[vmem((col_count,) + square, BF16)] * steps,
        *[vmem((row_count,) + square, BF16)] * steps,
        vmem((slots + 1,) + square, F32),
        vmem((slots + 1,) + square, F32),
        vmem((steps, 2, RING, RING - 1) + square, LT),
        vmem((steps, 2, RING, RING - 1) + square, LT),
        vmem((2,) + square, F32),
        vmem((steps, 2, RING - 1) + square, MT),
        vmem((steps, 2, RING - 1) + square, MT),
        vmem((steps,) + square, ZT),
        vmem((steps,) + square, ZT),
        vmem((steps, RING) + square, U1T),
        vmem((steps, RING) + square, U1T),
        vmem((steps, RING - 1) + square, U2T),
        vmem((steps, RING) + square, U2T),
        pltpu.SemaphoreType.DMA,
        pltpu.SemaphoreType.DMA,
        pltpu.SemaphoreType.DMA,
        pltpu.SemaphoreType.DMA((10,)),
        pltpu.SemaphoreType.DMA((27,)),
        pltpu.SemaphoreType.DMA((RING,)),
    ]
    smem = pl.BlockSpec(memory_space=pltpu.SMEM)
    whole = pl.BlockSpec(memory_space=pltpu.VMEM)

    hbm = pl.BlockSpec(memory_space=pl.ANY)
    result = jax.ShapeDtypeStruct(square, F32)
    shifted, previous = pl.pallas_call(
        kernel,
        out_shape=(result, result),
        in_specs=[smem, smem, smem, whole, whole, hbm, hbm],
        out_specs=(whole, whole),
        scratch_shapes=scratch,
        compiler_params=pltpu.CompilerParams(collective_id=0, has_side_effects=True),
        name="filter",
    )(block_counts, center, halfwidth, block_rows[0], block_cols[0], stacked, initial)
    return 2.0 * shifted - previous


def solution(mesh):
    in_specs = (
        P("row", "col", None, None, None),
        P("row", "col", None),
        P("row", "col", None),
        P("row", "col"),
        P(("row", "col"), None),
        P(),
        P(),
    )
    out_specs = P(("row", "col"), None)
    return jax.shard_map(body, mesh=mesh, in_specs=in_specs, out_specs=out_specs, check_vma=False)
```

```python
import jax
import jax.numpy as jnp
from jax import lax
from jax.experimental import pallas as pl
from jax.experimental.pallas import tpu as pltpu
from jax.sharding import PartitionSpec as P

DEGREE = 3
RING = 4
HALVES = 2
F32 = jnp.float32
BF16 = jnp.bfloat16
MESH = pl.DeviceIdType.MESH
GROUP = 32
AWAY = (2, 1, 3)

LT = BF16
MT = BF16
ZT = BF16
U1T = F32
U2T = BF16


U_BLOCK, U_PANEL, U_KEEP, U_END, L_BLOCK, L_PANEL, L_KEEP, L_END = range(8)


def order(key, payload, live, segments):
    slots = key.shape[1]
    square = (slots, slots)
    lane = lax.broadcasted_iota(jnp.int32, square, 1)
    slot = lax.broadcasted_iota(jnp.int32, square, 0)

    def upright(v):
        return jnp.sum(jnp.where(lane == slot, v, 0), axis=1, keepdims=True)

    def flat(mask, v):
        return jnp.sum(jnp.where(mask, v, 0), axis=0, keepdims=True)

    key = jnp.where(live, key, segments)
    payload = upright(jnp.where(live, payload, 0))
    mine = upright(key)
    before = (key < mine) | ((key == mine) & (lane < slot))
    rank = jnp.sum(before.astype(jnp.int32), axis=1, keepdims=True)
    hit = rank == lane
    keep = (flat(hit, mine) == flat(rank + 1 == lane, mine)) & (lane[:1] > 0)
    upto = flat(mine <= lane, 1)
    have = flat(mine == lane, 1)
    return [flat(hit, slot), flat(hit, payload), keep.astype(jnp.int32), jnp.where(have > 0, upto, 0)]


def kernel(
    counts,
    center,
    halfwidth,
    slot_rows,
    slot_cols,
    blocks_hbm,
    initial,
    out_shifted,
    out_previous,
    meta_vector,
    meta,
    blocks,
    current,
    previous,
    col0,
    col1,
    col2,
    row0,
    row1,
    row2,
    ups,
    lows,
    lsend,
    r1,
    msum,
    msend,
    r2,
    zsend,
    rz,
    usend1,
    ru1,
    usend2,
    ru2,
    load_sem,
    meta_sem,
    initial_sem,
    ssem,
    rsem,
    line_sem,
):
    slots, row_count, col_count = blocks.shape[0], row0.shape[0], col0.shape[0]
    grid_row = lax.axis_index("row")
    grid_col = lax.axis_index("col")
    core = grid_col % 2
    zl = grid_col // 2
    zh = grid_row % HALVES
    x = grid_row // HALVES % RING
    y = grid_row // (HALVES * RING)

    a = x * (1 - core) + y * core
    b = y * (1 - core) + x * core

    def row_of(da=0, db=0, dh=0):
        pa, pb = (a + da) % RING, (b + db) % RING
        px = pa * (1 - core) + pb * core
        py = pb * (1 - core) + pa * core
        return (py * RING + px) * HALVES + (zh + dh) % HALVES

    def place(da=0, db=0, dh=0):
        return (row_of(da, db, dh), grid_col)

    far_end = 3 * (1 - zl // 2)
    near = 1 + zl % 2
    along = (far_end, 6 - zl - far_end - near, near)

    def line(n):
        return (grid_row, along[n] * 2 + core)

    other_core = (grid_row, zl * 2 + 1 - core)

    barrier = pltpu.get_barrier_semaphore()
    peers = [other_core, place(dh=1)]
    peers += [place(da=d) for d in AWAY] + [place(db=d) for d in AWAY]
    peers += [line(n) for n in range(RING - 1)]
    for peer in peers:
        pl.semaphore_signal(barrier, inc=1, device_id=peer, device_id_type=MESH)
    first = pltpu.make_async_copy(initial, current, initial_sem)
    first.start()
    load = pltpu.make_async_copy(blocks_hbm, blocks, load_sem)
    load.start()
    nothing = jnp.zeros(current.shape, F32)
    ups[0] = nothing
    lows[0] = nothing
    live = lax.broadcasted_iota(jnp.int32, (1, slots), 1) < counts[0, 0]
    rows, cols = slot_rows[...], slot_cols[...]
    table = order(rows, cols, live, row_count) + order(cols, rows, live, col_count)
    meta_vector[...] = jnp.zeros_like(meta_vector)
    for n, entry in enumerate(table):
        meta_vector[n : n + 1, 0:slots] = entry
    order_copy = pltpu.make_async_copy(meta_vector, meta, meta_sem)
    order_copy.start()
    first.wait()
    pl.semaphore_wait(barrier, len(peers))

    send_ids, receive_ids = {}, {}

    def copy(leaves, arrives, src, dst, device, by_line=False):
        return pltpu.make_async_remote_copy(
            src_ref=src,
            dst_ref=dst,
            send_sem=ssem.at[send_ids.setdefault(leaves, len(send_ids))],
            recv_sem=line_sem.at[arrives] if by_line else rsem.at[receive_ids.setdefault(arrives, len(receive_ids))],
            device_id=device,
            device_id_type=MESH,
        )

    def wait(arrives, held, by_line=False):
        copy("z", arrives, held, held, other_core, by_line).wait_recv()

    def settle(leaves, held):
        copy(leaves, "z", held, held, other_core).wait_send()

    def settle_last(s):
        settle("mid", msend.at[s])
        settle("up", usend2.at[s])
        settle("back", zsend.at[s])

    def step(s):
        col, row = (col0, col1, col2)[s], (row0, row1, row2)[s]

        def send(leaves, arrives, src, dst, device, by_line=False):
            copy(leaves, arrives, src, dst, device, by_line).start()

        def panel(da=0, db=0, dh=0):
            return col.at[row_of(da, db, dh)]

        def spread1(dh):
            for d in AWAY:
                send("d1", f"d1.{dh}.{d}", panel(dh=dh), panel(dh=dh), place(da=d))

        def spread2(dh, da):
            for d in AWAY:
                held = panel(da=-da, dh=dh)
                send("d2", f"d2.{s}" if da or dh else "d2own", held, held, place(db=d))

        def pass2(dh, da):
            wait(f"d1.{dh}.{da}", panel(da=-da, dh=dh))
            spread2(dh, da)

        def row_at(z, which):
            return row.at[z * 2 + which]

        def row_pass(d):
            held = row_at(along[d], core)
            wait(along[d], held, True)
            send("pass", "pass", held, held, other_core)

        def low_end(da, db, dh):
            return meta[L_END, row_of(da, db, dh)]

        def reduce1_start(dh):
            for da in AWAY + (0,):
                for d in AWAY:
                    lsend[s, dh, da, d - 1] = lows[low_end(da, d, dh)].astype(LT)
                    send(
                        "low",
                        f"low.{dh}.{da}",
                        lsend.at[s, dh, da, d - 1],
                        r1.at[s, dh, da, d - 1],
                        place(db=d),
                    )

        def reduce1_end(dh, da):
            total = lows[low_end(da, 0, dh)]
            wait(f"low.{dh}.{da}", r1.at[s, dh, da])
            for d in AWAY:
                total = total + r1[s, dh, da, d - 1].astype(F32)
            if da == 0:
                msum[dh] = total
            else:
                msend[s, dh, da - 1] = total.astype(MT)
                send("mid", f"mid.{dh}", msend.at[s, dh, da - 1], r2.at[s, dh, da - 1], place(da=da))

        def reduce2_end(dh):
            total = msum[dh]
            wait(f"mid.{dh}", r2.at[s, dh])
            for d in AWAY:
                total = total + r2[s, dh, d - 1].astype(F32)
            return total

        now = current[...]
        col[row_of()] = now.astype(BF16)
        send("z", "z", panel(), panel(), place(dh=1))
        row[grid_col] = now.T.astype(BF16)
        for d in range(RING - 1):
            send("row", zl, row_at(zl, core), row_at(zl, core), line(d), True)
        send("pass", "pass", row_at(zl, core), row_at(zl, core), other_core)
        spread1(0)
        spread2(0, 0)
        pass2(0, 1)
        pass2(0, 3)
        row_pass(2)
        row_pass(1)
        pass2(0, 2)
        row_pass(0)
        wait("z", panel(dh=1))
        spread1(1)
        spread2(1, 0)
        wait("d2own", col.at[0 : RING - 1])
        wait("pass", row.at[0:RING])
        if s:
            settle_last(s - 1)
        if s == 0:
            order_copy.wait()
            load.wait()

        @pl.loop(0, slots // GROUP)
        def _(g):
            total = lows[g * GROUP]
            for i in range(GROUP):
                k = g * GROUP + i
                product = jnp.dot(
                    row[meta[L_PANEL, k]],
                    blocks[meta[L_BLOCK, k]],
                    preferred_element_type=F32,
                )
                total = product + meta[L_KEEP, k].astype(F32) * total
                lows[k + 1] = total

        reduce1_start(1)
        pass2(1, 1)
        pass2(1, 3)
        pass2(1, 2)
        reduce1_start(0)
        for db in AWAY + (0,):
            reduce1_end(1, db)
        wait(f"d2.{s}", col.at[0 : (2 * RING - 1) * (RING - 1)])

        @pl.loop(0, slots // GROUP)
        def _(g):
            total = ups[g * GROUP]
            for i in range(GROUP):
                k = g * GROUP + i
                product = jnp.dot(
                    blocks[meta[U_BLOCK, k]],
                    col[meta[U_PANEL, k]],
                    preferred_element_type=F32,
                )
                total = product + meta[U_KEEP, k].astype(F32) * total
                ups[k + 1] = total

        def up_end(z, which):
            return meta[U_END, z * 2 + which]

        for n, z in enumerate(along + (zl,)):
            usend1[s, z] = ups[up_end(z, 1 - core)].astype(U1T)
            send("chip", f"chip.{n}", usend1.at[s, z], ru1.at[s, z], other_core)
        zsend[s] = reduce2_end(1).astype(ZT)
        send("back", "back", zsend.at[s], rz.at[s], place(dh=1))
        for d in range(RING - 1):
            z = along[d]
            wait(f"chip.{d}", ru1.at[s, z])
            usend2[s, d] = (ups[up_end(z, core)] + ru1[s, z].astype(F32)).astype(U2T)
            send("up", "up", usend2.at[s, d], ru2.at[s, zl], line(d))
        wait(f"chip.{RING - 1}", ru1.at[s, zl])
        upper = ups[up_end(zl, core)] + ru1[s, zl].astype(F32)
        for db in AWAY + (0,):
            reduce1_end(0, db)
        settle("z", panel())
        settle("row", row.at[0 : RING - 1])
        settle("pass", row.at[0:RING])
        settle("d1", col.at[0 : 2 * (RING - 1)])
        settle("d2", col.at[0 : 2 * RING * (RING - 1)])
        settle("low", lsend.at[s])
        settle("chip", usend1.at[s])
        lower = reduce2_end(0)
        wait("up", ru2.at[s, 0 : RING - 1])
        for d in range(RING - 1):
            upper = upper + ru2[s, along[d]].astype(F32)
        wait("back", rz.at[s])
        lower = lower + rz[s].astype(F32)
        applied = upper + lower.T
        shifted = (applied - center[0] * now) / halfwidth[0]
        if s == DEGREE - 1:
            out_shifted[...] = shifted
            out_previous[...] = previous[...]
        else:
            following = shifted if s == 0 else 2.0 * shifted - previous[...]
            previous[...] = now
            current[...] = following

    for s in range(DEGREE):
        step(s)

    settle_last(DEGREE - 1)


def body(hamiltonian_blocks, block_rows, block_cols, block_counts, initial, center, halfwidth):
    stacked = hamiltonian_blocks[0, 0]
    slots, orbitals, _ = stacked.shape
    vectors = initial.shape[1]
    row_count = lax.axis_size("col")
    col_count = lax.axis_size("row")
    steps = DEGREE
    square = (orbitals, vectors)
    vmem = pltpu.VMEM
    scratch = [
        vmem((8, 128), jnp.int32),
        pltpu.SMEM((8, 128), jnp.int32),
        vmem((slots, orbitals, orbitals), BF16),
        vmem(square, F32),
        vmem(square, F32),
        *[vmem((col_count,) + square, BF16)] * steps,
        *[vmem((row_count,) + square, BF16)] * steps,
        vmem((slots + 1,) + square, F32),
        vmem((slots + 1,) + square, F32),
        vmem((steps, 2, RING, RING - 1) + square, LT),
        vmem((steps, 2, RING, RING - 1) + square, LT),
        vmem((2,) + square, F32),
        vmem((steps, 2, RING - 1) + square, MT),
        vmem((steps, 2, RING - 1) + square, MT),
        vmem((steps,) + square, ZT),
        vmem((steps,) + square, ZT),
        vmem((steps, RING) + square, U1T),
        vmem((steps, RING) + square, U1T),
        vmem((steps, RING - 1) + square, U2T),
        vmem((steps, RING) + square, U2T),
        pltpu.SemaphoreType.DMA,
        pltpu.SemaphoreType.DMA,
        pltpu.SemaphoreType.DMA,
        pltpu.SemaphoreType.DMA((10,)),
        pltpu.SemaphoreType.DMA((30,)),
        pltpu.SemaphoreType.DMA((RING,)),
    ]
    smem = pl.BlockSpec(memory_space=pltpu.SMEM)
    whole = pl.BlockSpec(memory_space=pltpu.VMEM)

    hbm = pl.BlockSpec(memory_space=pl.ANY)
    result = jax.ShapeDtypeStruct(square, F32)
    shifted, previous = pl.pallas_call(
        kernel,
        out_shape=(result, result),
        in_specs=[smem, smem, smem, whole, whole, hbm, hbm],
        out_specs=(whole, whole),
        scratch_shapes=scratch,
        compiler_params=pltpu.CompilerParams(collective_id=0, has_side_effects=True),
        name="filter",
    )(block_counts, center, halfwidth, block_rows[0], block_cols[0], stacked, initial)
    return 2.0 * shifted - previous


def solution(mesh):
    in_specs = (
        P("row", "col", None, None, None),
        P("row", "col", None),
        P("row", "col", None),
        P("row", "col"),
        P(("row", "col"), None),
        P(),
        P(),
    )
    out_specs = P(("row", "col"), None)
    return jax.shard_map(body, mesh=mesh, in_specs=in_specs, out_specs=out_specs, check_vma=False)
```
